32 devices in a mesh: tok: 8 (over y, x, core), feat: 4 (over z).
Axes of the slice: x: 2, y: 2, z: 4, core: 2. Of those that a mesh axis runs over, the one named last changes fastest.
Arguments:
- entering: bfloat16 [2560, 8192], P('feat', 'tok'), may hold values from -210 to 210
- leaving: bfloat16 [2560, 8192], P('feat', 'tok'), may hold values from -280 to 280
Outputs:
- transform: float32 [2560, 2560], P('feat', 'tok')
The draws below stay inside these ranges and needn't reach their ends.
All inputs are finite; a program needn't handle non-finite values.
Results may differ from the reference program's by a relative error of at most 0.00052.
Values may be sent and summed in bfloat16 or wider, within the bound.
A program may use at most 64 MiB of HBM per device.

```python
import math
import jax
import jax.numpy as jnp
from jax import lax

D = 2560
ITERS = 2
TOKENS = 8192


def common_pair(key):
    folded = jax.random.fold_in(key, 11)
    subkeys = jax.random.split(folded, 5)
    position = jnp.arange(TOKENS, dtype=jnp.float32)[:, None] / TOKENS
    feature_pos = jnp.arange(D, dtype=jnp.float32)[None, :] / D
    row_scale = jnp.exp(jax.random.uniform(subkeys[0], (TOKENS, 1), jnp.float32, 0.0, math.log(10.0)))
    row_scale = row_scale * jnp.exp(0.5 * math.log(10.0) * position)
    col_scale = jnp.exp(jax.random.uniform(subkeys[1], (1, D), jnp.float32, 0.0, math.log(10.0)))
    col_scale = col_scale * jnp.exp(0.5 * math.log(3.0) * feature_pos)
    residue = jax.random.normal(subkeys[4], (TOKENS, D), jnp.float32)
    pattern = jnp.clip(jax.random.normal(subkeys[2], (TOKENS, D), jnp.float32), -6.0, 6.0)
    residue = jnp.clip(residue, -6.0, 6.0)
    combined = row_scale * col_scale / 16.0
    entering = pattern * combined
    leaving = 0.8 * entering + 0.5 * residue * combined
    return (entering.T, leaving.T)


def draw_entering(key, part):
    return common_pair(key)[0].astype(jnp.bfloat16)


def draw_leaving(key, part):
    return common_pair(key)[1].astype(jnp.bfloat16)


def setup_inputs(seed: int = 0) -> dict:
    seeds = jax.random.split(jax.random.key(seed), 3)
    return {
        "entering": draw_entering(jax.random.fold_in(seeds[2], 71), 0),
        "leaving": draw_leaving(jax.random.fold_in(seeds[2], 71), 0),
    }


ridge_share = 0.2


def reference(entering, leaving):
    gram = jnp.dot(entering, entering.T, preferred_element_type=jnp.float32)
    cross = jnp.dot(entering, leaving.T, preferred_element_type=jnp.float32)
    energy = jnp.sum(jnp.square(entering.astype(jnp.float32)))
    ridge_term = ridge_share * energy / (TOKENS * D)
    upper_bound = jnp.max(jnp.sum(jnp.abs(gram), axis=1)) / TOKENS + ridge_term
    center = (upper_bound + ridge_term) / 2.0
    half_span = (upper_bound - ridge_term) / 2.0
    target = cross / TOKENS
    transform = target / center
    update = transform
    ratio_now = half_span / center
    for sweep in range(ITERS):
        iterate_half = lax.optimization_barrier(transform.astype(jnp.bfloat16))
        widened = iterate_half.astype(jnp.float32)
        applied = jnp.dot(gram, widened, precision=lax.Precision.HIGHEST)
        residual_now = target - (applied / TOKENS + ridge_term * widened)
        ratio_next = 1.0 / (2.0 * center / half_span - ratio_now)
        update = ratio_next * ratio_now * update + (2.0 * ratio_next / half_span) * residual_now
        transform = transform + update
        ratio_now = ratio_next
    return transform
```

```python
import functools

import jax
import jax.numpy as jnp
from jax import lax
from jax.experimental import pallas as pl
from jax.experimental.pallas import tpu as pltpu
from jax.sharding import PartitionSpec as P

ITERS = 2

ridge_share = 0.2

MESH = pl.DeviceIdType.MESH
VMEM_BYTES = 64000 * 1024


def token_product(left, right):
    return lax.dot_general(
        left, right, (((1,), (1,)), ((), ())), preferred_element_type=jnp.float32
    )


def plain_body(entering, leaving):
    row_count = entering.shape[0]
    order_all = row_count * lax.axis_size("feat")
    token_total = entering.shape[1] * lax.axis_size("tok")
    gram_piece = token_product(entering, lax.all_gather(entering, "feat", axis=0, tiled=True))
    cross_piece = token_product(entering, lax.all_gather(leaving, "feat", axis=0, tiled=True))
    gram_rows = lax.psum(gram_piece, "tok")
    cross_tile = lax.psum_scatter(cross_piece, "tok", scatter_dimension=1, tiled=True)
    row_peak = jnp.max(jnp.sum(jnp.abs(gram_rows), axis=1))
    own_squares = jnp.sum(jnp.square(entering.astype(jnp.float32)))
    energy = lax.psum(own_squares, ("tok", "feat"))
    peak_all = lax.pmax(row_peak, "feat")
    ridge_term = ridge_share * energy / (token_total * order_all)
    upper_bound = peak_all / token_total + ridge_term
    center = (upper_bound + ridge_term) / 2.0
    half_span = (upper_bound - ridge_term) / 2.0
    target = cross_tile / token_total
    transform = target / center
    update = transform
    ratio_now = half_span / center
    for sweep in range(ITERS):
        iterate_half = transform.astype(jnp.bfloat16)
        applied = jnp.dot(
            gram_rows,
            lax.all_gather(iterate_half, "feat", axis=0, tiled=True).astype(jnp.float32),
            precision=lax.Precision.HIGHEST,
        )
        residual_now = target - (
            applied / token_total + ridge_term * iterate_half.astype(jnp.float32)
        )
        ratio_next = 1.0 / (2.0 * center / half_span - ratio_now)
        update = ratio_next * ratio_now * update + 2.0 * ratio_next / half_span * residual_now
        transform = transform + update
        ratio_now = ratio_next
    return transform


def kernel(
    n_tok, n_feat,
    e_ref, l_ref, out_ref,
    eall, part, sib, recv, gall, glow, cbuf, ubuf, tbuf, tfull, stat, zstat, fin, halves, outs,
    load_sem, up_sem, down_sem, ag_sem, sib_ssem, sib_rsem, rs_ssem, rs_rsem,
    g_ssem, g_rsem, gl_ssem, gl_rsem, st_ssem, st_rsem, zs_ssem, zs_rsem,
    tg_ssem, tg_rsem, tf_ssem, tf_rsem, fa_ssem, fa_rsem, fb_ssem, fb_rsem,
):
    f32, bf16 = jnp.float32, jnp.bfloat16
    t = lax.axis_index("tok")
    z = lax.axis_index("feat")
    chips = n_tok // 2
    p, c = t // 2, t % 2
    mate = 2 * p + 1 - c
    rows, tokens = e_ref.shape
    sub = rows // n_tok
    token_total = tokens * n_tok
    order_all = rows * n_feat
    width = rows // 2

    load = pltpu.make_async_copy(e_ref, eall.at[z], load_sem)
    load.start()

    barrier = pltpu.get_barrier_semaphore()
    for d in range(1, n_tok):
        pl.semaphore_signal(
            barrier, inc=1, device_id=(lax.rem(t + d, n_tok), z), device_id_type=MESH
        )
    for d in range(1, n_feat):
        pl.semaphore_signal(
            barrier, inc=1, device_id=(t, lax.rem(z + d, n_feat)), device_id_type=MESH
        )
    load.wait()
    pl.semaphore_wait(barrier, n_tok + n_feat - 2)

    def remote(src, dst, ssem, rsem, tok, feat):
        return pltpu.make_async_remote_copy(
            src_ref=src, dst_ref=dst, send_sem=ssem, recv_sem=rsem,
            device_id=(tok, feat), device_id_type=MESH,
        )

    def up_copy(r):
        return remote(eall.at[r], eall.at[r], up_sem.at[r], ag_sem.at[r], t, z + 1)

    def down_copy(r):
        return remote(eall.at[r], eall.at[r], down_sem.at[r], ag_sem.at[r], t, z - 1)

    def sib_copy(r):
        return remote(part.at[r, 1 - c], sib.at[r], sib_ssem.at[r], sib_rsem.at[r], mate, z)

    def rs_copy(r, d):
        dest = lax.rem(p + d, chips)
        return remote(
            part.at[r, c, dest], recv.at[d - 1, r], rs_ssem.at[r, d - 1], rs_rsem.at[r, d - 1],
            2 * dest + c, z,
        )

    def fetch(r, first):
        @pl.when(jnp.logical_not(first))
        def _():
            down_copy(r).wait_recv()

        @pl.when(jnp.logical_and(r <= z, z < n_feat - 1))
        def _():
            up_copy(r).start()

        @pl.when(jnp.logical_and(r >= z, z > 0))
        def _():
            down_copy(r).start()

    def process(r):
        def chip_rows(q, carry):
            at = pl.multiple_of(q * 2 * sub, 2 * sub)
            block = eall[r, pl.ds(at, 2 * sub), :]
            gram = token_product(block, e_ref[...])
            part[r, 0, q, 0] = gram[:sub]
            part[r, 1, q, 0] = gram[sub:]
            cross = token_product(block, l_ref[...])
            part[r, 0, q, 1] = cross[:sub]
            part[r, 1, q, 1] = cross[sub:]
            return carry

        lax.fori_loop(0, chips, chip_rows, 0)
        sib_copy(r).start()

    def finish(r):
        sib_copy(r).wait_recv()

        def add(q, carry):
            part[r, c, q] = part[r, c, q] + sib[r, q]
            return carry

        lax.fori_loop(0, chips, add, 0)
        for d in range(1, chips):
            rs_copy(r, d).start()

    def both(s, action):
        @pl.when(z - s >= 0)
        def _():
            action(z - s)

        @pl.when(jnp.logical_and(s > 0, z + s < n_feat))
        def _():
            action(z + s)

    def level(s, carry):
        both(s, lambda r: fetch(r, s == 0))
        both(s, process)

        @pl.when(s > 0)
        def _():
            both(s - 1, finish)

        return carry

    lax.fori_loop(0, n_feat, level, 0)
    both(n_feat - 1, finish)

    col_abs = jnp.zeros((8, rows), f32)
    diag = jnp.zeros((8, rows), f32)
    row_id = lax.broadcasted_iota(jnp.int32, (sub, rows), 0)
    col_id = lax.broadcasted_iota(jnp.int32, (sub, rows), 1)
    on_diag = col_id == row_id + t * sub

    def total(r, carry):
        col_abs, diag = carry
        for d in range(1, chips):
            rs_copy(r, d).wait_recv()
        both_sum = part[r, c, p]
        for d in range(1, chips):
            both_sum = both_sum + recv[d - 1, r]
        gram = both_sum[0]
        cbuf[r] = both_sum[1] / token_total
        high = gram.astype(bf16)
        gall[z, r] = high

        @pl.when(r == z)
        def _():
            glow[z] = (gram - high.astype(f32)).astype(bf16)

        col_abs = col_abs + jnp.sum(jnp.abs(gram).reshape(sub // 8, 8, rows), axis=0)
        kept = jnp.where(on_diag, gram, 0.0) * jnp.where(r == z, 1.0, 0.0)
        diag = diag + jnp.sum(kept.reshape(sub // 8, 8, rows), axis=0)
        return col_abs, diag

    col_abs, diag = lax.fori_loop(0, n_feat, total, (col_abs, diag))
    stat[t, 0] = col_abs
    stat[t, 1] = diag

    def st_copy(d):
        return remote(
            stat.at[t], stat.at[t], st_ssem.at[d - 1], st_rsem.at[d - 1],
            lax.rem(t + d, n_tok), z,
        )

    def g_copy(d):
        return remote(
            gall.at[z], gall.at[z], g_ssem.at[d - 1], g_rsem.at[d - 1],
            t, lax.rem(z + d, n_feat),
        )

    def gl_copy(d):
        return remote(
            glow.at[z], glow.at[z], gl_ssem.at[d - 1], gl_rsem.at[d - 1],
            t, lax.rem(z + d, n_feat),
        )

    def zs_copy(d):
        return remote(
            zstat.at[z], zstat.at[z], zs_ssem.at[d - 1], zs_rsem.at[d - 1],
            t, lax.rem(z + d, n_feat),
        )

    for d in range(1, n_tok):
        st_copy(d).start()
    for d in range(1, n_tok):
        st_copy(d).wait_recv()
    tok_sum = jnp.sum(stat[...], axis=0)
    sums = jnp.sum(tok_sum[0], axis=0, keepdims=True)
    peak = jnp.max(sums, axis=1, keepdims=True)
    trace = jnp.sum(jnp.sum(tok_sum[1], axis=0, keepdims=True), axis=1, keepdims=True)
    zstat[z, 0] = jnp.broadcast_to(peak, (8, 128))
    zstat[z, 1] = jnp.broadcast_to(trace, (8, 128))
    for d in range(1, n_feat):
        zs_copy(d).start()
    for d in range(1, n_feat):
        g_copy(d).start()
        gl_copy(d).start()
    for d in range(1, n_feat):
        zs_copy(d).wait_recv()
    seen = zstat[...]
    peak_all = jnp.max(seen[:, 0], axis=0)[:1, :1]
    energy = jnp.sum(seen[:, 1], axis=0)[:1, :1]
    ridge_term = ridge_share * energy / (token_total * order_all)
    upper_bound = peak_all / token_total + ridge_term
    center = (upper_bound + ridge_term) / 2.0
    half_span = (upper_bound - ridge_term) / 2.0
    ratio_now = half_span / center

    def start_iterate(r, carry):
        first = cbuf[r] / center
        tbuf[r] = first
        ubuf[r] = first
        tfull[0, r, t] = first.astype(bf16)
        return carry

    lax.fori_loop(0, n_feat, start_iterate, 0)

    def tg_copy(it, d):
        dest = lax.rem(p + d, chips)
        return remote(
            tfull.at[it, :, t], tfull.at[it, :, t], tg_ssem.at[it, d - 1], tg_rsem.at[it, d - 1],
            2 * dest + c, z,
        )

    def tf_copy(it, d):
        tile = 2 * lax.rem(p + chips - d, chips) + c
        return remote(
            tfull.at[it, :, tile], tfull.at[it, :, tile], tf_ssem.at[it, d], tf_rsem.at[it, d],
            mate, z,
        )

    for it in range(ITERS):
        for d in range(1, chips):
            tg_copy(it, d).start()
        tf_copy(it, 0).start()
        for d in range(1, chips):
            tg_copy(it, d).wait_recv()
            tf_copy(it, d).start()
        if it == 0:
            for d in range(1, n_feat):
                g_copy(d).wait_recv()
                gl_copy(d).wait_recv()
        for d in range(chips):
            tf_copy(it, d).wait_recv()
        ratio_next = 1.0 / (2.0 * center / half_span - ratio_now)
        keep = ratio_next * ratio_now
        gain = 2.0 * ratio_next / half_span

        def multiply(k, carry):
            weights = tfull[it, k].reshape(rows, rows)
            left = gall[k].reshape(n_feat * sub, rows)
            product = jnp.dot(left, weights, preferred_element_type=f32)
            low = jnp.dot(glow[k], weights, preferred_element_type=f32)
            product = product.reshape(n_feat, sub, rows)

            @pl.when(k == 0)
            def _():
                fin[...] = product

            @pl.when(k > 0)
            def _():
                fin[...] = fin[...] + product

            recv[0, k, 0] = low
            return carry

        lax.fori_loop(0, n_feat, multiply, 0)

        def advance(r, carry):
            applied = fin[r] + recv[0, r, 0]
            half = tfull[it, r, t].astype(f32)
            residual = cbuf[r] - (applied / token_total + ridge_term * half)
            update = keep * ubuf[r] + gain * residual
            after = tbuf[r] + update
            ubuf[r] = update
            tbuf[r] = after
            if it + 1 < ITERS:
                tfull[it + 1, r, t] = after.astype(bf16)
            return carry

        lax.fori_loop(0, n_feat, advance, 0)
        ratio_now = ratio_next

    def fa_copy(d):
        dest = lax.rem(z + d, n_feat)
        return remote(
            tbuf.at[dest], sib.at[0, z, 0], fa_ssem.at[d - 1], fa_rsem.at[d - 1], t, dest
        )

    def fb_copy(d):
        dest = lax.rem(t + d, n_tok)
        return remote(
            halves.at[dest], outs.at[t], fb_ssem.at[d - 1], fb_rsem.at[d - 1], dest, z
        )

    for d in range(1, n_feat):
        fa_copy(d).start()
    sib[0, z, 0] = tbuf[z]
    for d in range(1, n_feat):
        fa_copy(d).wait_recv()
    for k in range(n_feat):
        tile = sib[0, k, 0]
        halves[2 * k] = tile[:, :width]
        halves[2 * k + 1] = tile[:, width:]
    for d in range(1, n_tok):
        fb_copy(d).start()
    outs[t] = halves[t]
    for d in range(1, n_tok):
        fb_copy(d).wait_recv()
    out_ref[...] = outs[...]

    def drain(r, carry):
        @pl.when(jnp.logical_and(r <= z, z < n_feat - 1))
        def _():
            up_copy(r).wait_send()

        @pl.when(jnp.logical_and(r >= z, z > 0))
        def _():
            down_copy(r).wait_send()

        sib_copy(r).wait_send()
        for d in range(1, chips):
            rs_copy(r, d).wait_send()
        return carry

    lax.fori_loop(0, n_feat, drain, 0)
    for d in range(1, n_tok):
        st_copy(d).wait_send()
        fb_copy(d).wait_send()
    for d in range(1, n_feat):
        g_copy(d).wait_send()
        gl_copy(d).wait_send()
        zs_copy(d).wait_send()
        fa_copy(d).wait_send()
    for it in range(ITERS):
        for d in range(1, chips):
            tg_copy(it, d).wait_send()
        for d in range(chips):
            tf_copy(it, d).wait_send()


def kernel_body(n_tok, n_feat, entering, leaving):
    rows, tokens = entering.shape
    chips, sub, width = n_tok // 2, rows // n_tok, rows // 2
    f32, bf16 = jnp.float32, jnp.bfloat16
    dma = pltpu.SemaphoreType.DMA
    vmem = pltpu.VMEM
    tile = (n_feat, sub, rows)
    out = pl.pallas_call(
        functools.partial(kernel, n_tok, n_feat),
        out_shape=jax.ShapeDtypeStruct((n_tok, sub, width), f32),
        in_specs=[pl.BlockSpec(memory_space=pltpu.VMEM)] * 2,
        out_specs=pl.BlockSpec(memory_space=pltpu.VMEM),
        scratch_shapes=[
            vmem((n_feat, rows, tokens), bf16),
            vmem((n_feat, 2, chips, 2, sub, rows), f32),
            vmem((n_feat, chips, 2, sub, rows), f32),
            vmem((chips - 1, n_feat, 2, sub, rows), f32),
            vmem((n_feat, n_feat, sub, rows), bf16),
            vmem((n_feat, sub, rows), bf16),
            vmem(tile, f32),
            vmem(tile, f32),
            vmem(tile, f32),
            vmem((ITERS, n_feat, n_tok, sub, rows), bf16),
            vmem((n_tok, 2, 8, rows), f32),
            vmem((n_feat, 2, 8, 128), f32),
            vmem(tile, f32),
            vmem((n_tok, sub, width), f32),
            vmem((n_tok, sub, width), f32),
            dma,
            dma((n_feat,)), dma((n_feat,)), dma((n_feat,)),
            dma((n_feat,)), dma((n_feat,)),
            dma((n_feat, chips - 1)), dma((n_feat, chips - 1)),
            dma((n_feat - 1,)), dma((n_feat - 1,)),
            dma((n_feat - 1,)), dma((n_feat - 1,)),
            dma((n_tok - 1,)), dma((n_tok - 1,)),
            dma((n_feat - 1,)), dma((n_feat - 1,)),
            dma((ITERS, chips - 1)), dma((ITERS, chips - 1)),
            dma((ITERS, chips)), dma((ITERS, chips)),
            dma((n_feat - 1,)), dma((n_feat - 1,)),
            dma((n_tok - 1,)), dma((n_tok - 1,)),
        ],
        compiler_params=pltpu.CompilerParams(
            collective_id=0, has_side_effects=True, vmem_limit_bytes=VMEM_BYTES
        ),
    )(entering, leaving)
    return out.reshape(rows, width)


def solution(mesh):
    n_tok, n_feat = mesh.shape["tok"], mesh.shape["feat"]

    def body(entering, leaving):
        rows, tokens = entering.shape
        fits = (
            n_tok == 2 * n_feat
            and rows % (16 * n_tok) == 0
            and rows % 128 == 0
            and tokens % 128 == 0
        )
        if fits:
            return kernel_body(n_tok, n_feat, entering, leaving)
        return plain_body(entering, leaving)

    in_specs = (P("feat", "tok"), P("feat", "tok"))
    out_specs = P("feat", "tok")
    return jax.shard_map(body, mesh=mesh, in_specs=in_specs, out_specs=out_specs, check_vma=False)
```

```python
import functools

import jax
import jax.numpy as jnp
from jax import lax
from jax.experimental import pallas as pl
from jax.experimental.pallas import tpu as pltpu
from jax.sharding import PartitionSpec as P

ITERS = 2

ridge_share = 0.2

MESH = pl.DeviceIdType.MESH
VMEM_BYTES = 64000 * 1024


def token_product(left, right):
    return lax.dot_general(
        left, right, (((1,), (1,)), ((), ())), preferred_element_type=jnp.float32
    )


def plain_body(entering, leaving):
    row_count = entering.shape[0]
    order_all = row_count * lax.axis_size("feat")
    token_total = entering.shape[1] * lax.axis_size("tok")
    gram_piece = token_product(entering, lax.all_gather(entering, "feat", axis=0, tiled=True))
    cross_piece = token_product(entering, lax.all_gather(leaving, "feat", axis=0, tiled=True))
    gram_rows = lax.psum(gram_piece, "tok")
    cross_tile = lax.psum_scatter(cross_piece, "tok", scatter_dimension=1, tiled=True)
    row_peak = jnp.max(jnp.sum(jnp.abs(gram_rows), axis=1))
    own_squares = jnp.sum(jnp.square(entering.astype(jnp.float32)))
    energy = lax.psum(own_squares, ("tok", "feat"))
    peak_all = lax.pmax(row_peak, "feat")
    ridge_term = ridge_share * energy / (token_total * order_all)
    upper_bound = peak_all / token_total + ridge_term
    center = (upper_bound + ridge_term) / 2.0
    half_span = (upper_bound - ridge_term) / 2.0
    target = cross_tile / token_total
    transform = target / center
    update = transform
    ratio_now = half_span / center
    for sweep in range(ITERS):
        iterate_half = transform.astype(jnp.bfloat16)
        applied = jnp.dot(
            gram_rows,
            lax.all_gather(iterate_half, "feat", axis=0, tiled=True).astype(jnp.float32),
            precision=lax.Precision.HIGHEST,
        )
        residual_now = target - (
            applied / token_total + ridge_term * iterate_half.astype(jnp.float32)
        )
        ratio_next = 1.0 / (2.0 * center / half_span - ratio_now)
        update = ratio_next * ratio_now * update + 2.0 * ratio_next / half_span * residual_now
        transform = transform + update
        ratio_now = ratio_next
    return transform


def kernel(
    n_tok, n_feat,
    e_ref, l_ref, out_ref,
    eall, part, sib, recv, gall, glow, cbuf, ubuf, tbuf, tfull, stat, zstat, fin, halves, outs,
    load_sem, up_sem, down_sem, ag_sem, sib_ssem, sib_rsem, rs_ssem, rs_rsem,
    g_ssem, g_rsem, gl_ssem, gl_rsem, st_ssem, st_rsem, zs_ssem, zs_rsem,
    tg_ssem, tg_rsem, tf_ssem, tf_rsem, fa_ssem, fa_rsem, fb_ssem, fb_rsem,
):
    f32, bf16 = jnp.float32, jnp.bfloat16
    t = lax.axis_index("tok")
    z = lax.axis_index("feat")
    chips = n_tok // 2
    p, c = t // 2, t % 2
    mate = 2 * p + 1 - c
    sub, tokens = e_ref.shape[1:]
    rows = sub * n_tok
    cut = 16 * ((sub // 16 + 1) // 2)
    pieces = [(0, cut), (cut, sub)]
    group = 2 if chips % 2 == 0 else 1
    token_total = tokens * n_tok
    order_all = rows * n_feat
    width = rows // 2

    load = pltpu.make_async_copy(e_ref, eall.at[z], load_sem)
    load.start()

    barrier = pltpu.get_barrier_semaphore()
    for d in range(1, n_tok):
        pl.semaphore_signal(
            barrier, inc=1, device_id=(lax.rem(t + d, n_tok), z), device_id_type=MESH
        )
    for d in range(1, n_feat):
        pl.semaphore_signal(
            barrier, inc=1, device_id=(t, lax.rem(z + d, n_feat)), device_id_type=MESH
        )
    load.wait()
    pl.semaphore_wait(barrier, n_tok + n_feat - 2)

    def remote(src, dst, ssem, rsem, tok, feat):
        return pltpu.make_async_remote_copy(
            src_ref=src, dst_ref=dst, send_sem=ssem, recv_sem=rsem,
            device_id=(tok, feat), device_id_type=MESH,
        )

    def up_copy(r, h):
        at = eall.at[r, :, slice(*pieces[h])]
        return remote(at, at, up_sem.at[r, h], ag_sem.at[r, h], t, z + 1)

    def down_copy(r, h):
        at = eall.at[r, :, slice(*pieces[h])]
        return remote(at, at, down_sem.at[r, h], ag_sem.at[r, h], t, z - 1)

    def sib_copy(r, h):
        at = slice(*pieces[h])
        return remote(
            part.at[r, 1 - c, :, :, at], sib.at[r, :, :, at], sib_ssem.at[r, h],
            sib_rsem.at[r, h], mate, z,
        )

    def rs_copy(r, h, d):
        dest = lax.rem(p + d, chips)
        at = slice(*pieces[h])
        return remote(
            part.at[r, c, dest, :, at], recv.at[d - 1, r, :, at], rs_ssem.at[r, h, d - 1],
            rs_rsem.at[r, h, d - 1], 2 * dest + c, z,
        )

    def g_copy(r, d):
        return remote(
            gall.at[z, r], gall.at[z, r], g_ssem.at[r, d - 1], g_rsem.at[r, d - 1],
            t, lax.rem(z + d, n_feat),
        )

    def gl_copy(d):
        return remote(
            glow.at[z], glow.at[z], gl_ssem.at[d - 1], gl_rsem.at[d - 1],
            t, lax.rem(z + d, n_feat),
        )

    def fetch(r, h, first):
        @pl.when(jnp.logical_not(first))
        def _():
            down_copy(r, h).wait_recv()

        @pl.when(jnp.logical_and(r <= z, z < n_feat - 1))
        def _():
            up_copy(r, h).start()

        @pl.when(jnp.logical_and(r >= z, z > 0))
        def _():
            down_copy(r, h).start()

    def process(r, h):
        lo, hi = pieces[h]
        size = hi - lo
        own_e = e_ref[...].reshape(rows, tokens)

        def chip_rows(k, carry):
            block = eall[r, pl.ds(k * 2 * group, 2 * group), lo:hi, :]
            block = block.reshape(2 * group * size, tokens)
            gram = token_product(block, own_e)
            cross = token_product(block, l_ref[...])
            for g in range(group):
                for core in range(2):
                    at = (2 * g + core) * size
                    part[r, core, k * group + g, 0, lo:hi] = gram[at : at + size]
                    part[r, core, k * group + g, 1, lo:hi] = cross[at : at + size]
            return carry

        lax.fori_loop(0, chips // group, chip_rows, 0)
        sib_copy(r, h).start()

    def finish(r, h):
        lo, hi = pieces[h]
        sib_copy(r, h).wait_recv()

        def add(q, carry):
            part[r, c, q, :, lo:hi] = part[r, c, q, :, lo:hi] + sib[r, q, :, lo:hi]
            return carry

        lax.fori_loop(0, chips, add, 0)
        for d in range(1, chips):
            rs_copy(r, h, d).start()

    def both(s, action):
        @pl.when(z - s >= 0)
        def _():
            action(z - s)

        @pl.when(jnp.logical_and(s > 0, z + s < n_feat))
        def _():
            action(z + s)

    def level(s, carry):
        both(s, lambda r: fetch(r, 0, s == 0))
        both(s, lambda r: process(r, 0))

        @pl.when(s > 0)
        def _():
            both(s - 1, lambda r: finish(r, 1))

        both(s, lambda r: fetch(r, 1, s == 0))
        both(s, lambda r: process(r, 1))
        both(s, lambda r: finish(r, 0))
        return carry

    lax.fori_loop(0, n_feat, level, 0)

    stat[t] = jnp.zeros((8, rows), f32)

    row_id = lax.broadcasted_iota(jnp.int32, (sub, rows), 0)
    col_id = lax.broadcasted_iota(jnp.int32, (sub, rows), 1)
    on_diag = col_id == row_id + t * sub

    def total(r):
        for h in range(len(pieces)):
            for d in range(1, chips):
                rs_copy(r, h, d).wait_recv()
        both_sum = part[r, c, p]
        for d in range(1, chips):
            both_sum = both_sum + recv[d - 1, r]
        gram = both_sum[0]
        cbuf[r] = both_sum[1] / token_total
        high = gram.astype(bf16)
        gall[z, r] = high
        for d in range(1, n_feat):
            g_copy(r, d).start()

        @pl.when(r == z)
        def _():
            glow[z] = (gram - high.astype(f32)).astype(bf16)
            for d in range(1, n_feat):
                gl_copy(d).start()

        stat[t, 0:1] += jnp.sum(jnp.abs(gram), axis=0, keepdims=True)
        kept = jnp.where(on_diag, gram, 0.0) * jnp.where(r == z, 1.0, 0.0)
        stat[t, 1:2] += jnp.sum(kept, axis=0, keepdims=True)

    def early(s, carry):
        both(s, total)
        return carry

    lax.fori_loop(0, n_feat - 1, early, 0)
    both(n_feat - 1, lambda r: finish(r, 1))
    both(n_feat - 1, total)

    def st_copy(d):
        return remote(
            stat.at[t], stat.at[t], st_ssem.at[d - 1], st_rsem.at[d - 1],
            lax.rem(t + d, n_tok), z,
        )

    def zs_copy(d):
        return remote(
            zstat.at[z], zstat.at[z], zs_ssem.at[d - 1], zs_rsem.at[d - 1],
            t, lax.rem(z + d, n_feat),
        )

    for d in range(1, n_tok):
        st_copy(d).start()
    for d in range(1, n_tok):
        st_copy(d).wait_recv()
    tok_sum = jnp.sum(stat[...], axis=0)
    peak = jnp.max(tok_sum[0:1], axis=1, keepdims=True)
    trace = jnp.sum(tok_sum[1:2], axis=1, keepdims=True)
    zstat[z, 0] = jnp.broadcast_to(peak, (8, 128))
    zstat[z, 1] = jnp.broadcast_to(trace, (8, 128))
    for d in range(1, n_feat):
        zs_copy(d).start()
    for d in range(1, n_feat):
        zs_copy(d).wait_recv()
    seen = zstat[...]
    peak_all = jnp.max(seen[:, 0], axis=0)[:1, :1]
    energy = jnp.sum(seen[:, 1], axis=0)[:1, :1]
    ridge_term = ridge_share * energy / (token_total * order_all)
    upper_bound = peak_all / token_total + ridge_term
    center = (upper_bound + ridge_term) / 2.0
    half_span = (upper_bound - ridge_term) / 2.0
    ratio_now = half_span / center

    def start_iterate(r, carry):
        first = cbuf[r] / center
        tbuf[r] = first
        ubuf[r] = first
        tfull[0, r, t] = first.astype(bf16)
        return carry

    lax.fori_loop(0, n_feat, start_iterate, 0)

    def tg_copy(it, d):
        dest = lax.rem(p + d, chips)
        return remote(
            tfull.at[it, :, t], tfull.at[it, :, t], tg_ssem.at[it, d - 1], tg_rsem.at[it, d - 1],
            2 * dest + c, z,
        )

    def tf_copy(it, d):
        tile = 2 * lax.rem(p + chips - d, chips) + c
        return remote(
            tfull.at[it, :, tile], tfull.at[it, :, tile], tf_ssem.at[it, d], tf_rsem.at[it, d],
            mate, z,
        )

    for it in range(ITERS):
        for d in range(1, chips):
            tg_copy(it, d).start()
        tf_copy(it, 0).start()
        for d in range(1, chips):
            tg_copy(it, d).wait_recv()
            tf_copy(it, d).start()
        if it == 0:
            for d in range(1, n_feat):
                for r in range(n_feat):
                    g_copy(r, d).wait_recv()
                gl_copy(d).wait_recv()
        for d in range(chips):
            tf_copy(it, d).wait_recv()
        ratio_next = 1.0 / (2.0 * center / half_span - ratio_now)
        keep = ratio_next * ratio_now
        gain = 2.0 * ratio_next / half_span

        def multiply(k, carry):
            weights = tfull[it, k].reshape(rows, rows)
            left = gall[k].reshape(n_feat * sub, rows)
            product = jnp.dot(left, weights, preferred_element_type=f32)
            low = jnp.dot(glow[k], weights, preferred_element_type=f32)
            product = product.reshape(n_feat, sub, rows)

            @pl.when(k == 0)
            def _():
                fin[...] = product

            @pl.when(k > 0)
            def _():
                fin[...] = fin[...] + product

            recv[0, k, 0] = low
            return carry

        lax.fori_loop(0, n_feat, multiply, 0)

        def advance(r, carry):
            applied = fin[r] + recv[0, r, 0]
            half = tfull[it, r, t].astype(f32)
            residual = cbuf[r] - (applied / token_total + ridge_term * half)
            update = keep * ubuf[r] + gain * residual
            after = tbuf[r] + update
            ubuf[r] = update
            tbuf[r] = after
            if it + 1 < ITERS:
                tfull[it + 1, r, t] = after.astype(bf16)
            return carry

        lax.fori_loop(0, n_feat, advance, 0)
        ratio_now = ratio_next

    def fa_copy(d):
        dest = lax.rem(z + d, n_feat)
        return remote(
            tbuf.at[dest], sib.at[0, z, 0], fa_ssem.at[d - 1], fa_rsem.at[d - 1], t, dest
        )

    def fb_copy(d):
        dest = lax.rem(t + d, n_tok)
        return remote(
            halves.at[dest], outs.at[t], fb_ssem.at[d - 1], fb_rsem.at[d - 1], dest, z
        )

    for d in range(1, n_feat):
        fa_copy(d).start()
    sib[0, z, 0] = tbuf[z]
    for d in range(1, n_feat):
        fa_copy(d).wait_recv()
    for k in range(n_feat):
        tile = sib[0, k, 0]
        halves[2 * k] = tile[:, :width]
        halves[2 * k + 1] = tile[:, width:]
    for d in range(1, n_tok):
        fb_copy(d).start()
    outs[t] = halves[t]
    for d in range(1, n_tok):
        fb_copy(d).wait_recv()
    out_ref[...] = outs[...]

    def drain(r, carry):
        for h in range(len(pieces)):
            @pl.when(jnp.logical_and(r <= z, z < n_feat - 1))
            def _():
                up_copy(r, h).wait_send()

            @pl.when(jnp.logical_and(r >= z, z > 0))
            def _():
                down_copy(r, h).wait_send()

            sib_copy(r, h).wait_send()
            for d in range(1, chips):
                rs_copy(r, h, d).wait_send()
        for d in range(1, n_feat):
            g_copy(r, d).wait_send()
        return carry

    lax.fori_loop(0, n_feat, drain, 0)
    for d in range(1, n_tok):
        st_copy(d).wait_send()
        fb_copy(d).wait_send()
    for d in range(1, n_feat):
        gl_copy(d).wait_send()
        zs_copy(d).wait_send()
        fa_copy(d).wait_send()
    for it in range(ITERS):
        for d in range(1, chips):
            tg_copy(it, d).wait_send()
        for d in range(chips):
            tf_copy(it, d).wait_send()


def kernel_body(n_tok, n_feat, entering, leaving):
    rows, tokens = entering.shape
    chips, sub, width = n_tok // 2, rows // n_tok, rows // 2
    f32, bf16 = jnp.float32, jnp.bfloat16
    dma = pltpu.SemaphoreType.DMA
    vmem = pltpu.VMEM
    tile = (n_feat, sub, rows)
    out = pl.pallas_call(
        functools.partial(kernel, n_tok, n_feat),
        out_shape=jax.ShapeDtypeStruct((n_tok, sub, width), f32),
        in_specs=[pl.BlockSpec(memory_space=pltpu.VMEM)] * 2,
        out_specs=pl.BlockSpec(memory_space=pltpu.VMEM),
        scratch_shapes=[
            vmem((n_feat, n_tok, sub, tokens), bf16),
            vmem((n_feat, 2, chips, 2, sub, rows), f32),
            vmem((n_feat, chips, 2, sub, rows), f32),
            vmem((chips - 1, n_feat, 2, sub, rows), f32),
            vmem((n_feat, n_feat, sub, rows), bf16),
            vmem((n_feat, sub, rows), bf16),
            vmem(tile, f32),
            vmem(tile, f32),
            vmem(tile, f32),
            vmem((ITERS, n_feat, n_tok, sub, rows), bf16),
            vmem((n_tok, 8, rows), f32),
            vmem((n_feat, 2, 8, 128), f32),
            vmem(tile, f32),
            vmem((n_tok, sub, width), f32),
            vmem((n_tok, sub, width), f32),
            dma,
            dma((n_feat, 2)), dma((n_feat, 2)), dma((n_feat, 2)),
            dma((n_feat, 2)), dma((n_feat, 2)),
            dma((n_feat, 2, chips - 1)), dma((n_feat, 2, chips - 1)),
            dma((n_feat, n_feat - 1)), dma((n_feat, n_feat - 1)),
            dma((n_feat - 1,)), dma((n_feat - 1,)),
            dma((n_tok - 1,)), dma((n_tok - 1,)),
            dma((n_feat - 1,)), dma((n_feat - 1,)),
            dma((ITERS, chips - 1)), dma((ITERS, chips - 1)),
            dma((ITERS, chips)), dma((ITERS, chips)),
            dma((n_feat - 1,)), dma((n_feat - 1,)),
            dma((n_tok - 1,)), dma((n_tok - 1,)),
        ],
        compiler_params=pltpu.CompilerParams(
            collective_id=0, has_side_effects=True, vmem_limit_bytes=VMEM_BYTES
        ),
    )(entering.reshape(n_tok, sub, tokens), leaving)
    return out.reshape(rows, width)


def solution(mesh):
    n_tok, n_feat = mesh.shape["tok"], mesh.shape["feat"]

    def body(entering, leaving):
        rows, tokens = entering.shape
        fits = (
            n_tok == 2 * n_feat
            and rows % (32 * n_tok) in (0, 16 * n_tok)
            and rows // n_tok > 16
            and rows % 128 == 0
            and tokens % 128 == 0
        )
        if fits:
            return kernel_body(n_tok, n_feat, entering, leaving)
        return plain_body(entering, leaving)

    in_specs = (P("feat", "tok"), P("feat", "tok"))
    out_specs = P("feat", "tok")
    return jax.shard_map(body, mesh=mesh, in_specs=in_specs, out_specs=out_specs, check_vma=False)
```

```python
import functools

import jax
import jax.numpy as jnp
from jax import lax
from jax.experimental import pallas as pl
from jax.experimental.pallas import tpu as pltpu
from jax.sharding import PartitionSpec as P

ITERS = 2

ridge_share = 0.2

MESH = pl.DeviceIdType.MESH
VMEM_BYTES = 64000 * 1024


def token_product(left, right):
    return lax.dot_general(
        left, right, (((1,), (1,)), ((), ())), preferred_element_type=jnp.float32
    )


def plain_body(entering, leaving):
    row_count = entering.shape[0]
    order_all = row_count * lax.axis_size("feat")
    token_total = entering.shape[1] * lax.axis_size("tok")
    gram_piece = token_product(entering, lax.all_gather(entering, "feat", axis=0, tiled=True))
    cross_piece = token_product(entering, lax.all_gather(leaving, "feat", axis=0, tiled=True))
    gram_rows = lax.psum(gram_piece, "tok")
    cross_tile = lax.psum_scatter(cross_piece, "tok", scatter_dimension=1, tiled=True)
    row_peak = jnp.max(jnp.sum(jnp.abs(gram_rows), axis=1))
    own_squares = jnp.sum(jnp.square(entering.astype(jnp.float32)))
    energy = lax.psum(own_squares, ("tok", "feat"))
    peak_all = lax.pmax(row_peak, "feat")
    ridge_term = ridge_share * energy / (token_total * order_all)
    upper_bound = peak_all / token_total + ridge_term
    center = (upper_bound + ridge_term) / 2.0
    half_span = (upper_bound - ridge_term) / 2.0
    target = cross_tile / token_total
    transform = target / center
    update = transform
    ratio_now = half_span / center
    for sweep in range(ITERS):
        iterate_half = transform.astype(jnp.bfloat16)
        applied = jnp.dot(
            gram_rows,
            lax.all_gather(iterate_half, "feat", axis=0, tiled=True).astype(jnp.float32),
            precision=lax.Precision.HIGHEST,
        )
        residual_now = target - (
            applied / token_total + ridge_term * iterate_half.astype(jnp.float32)
        )
        ratio_next = 1.0 / (2.0 * center / half_span - ratio_now)
        update = ratio_next * ratio_now * update + 2.0 * ratio_next / half_span * residual_now
        transform = transform + update
        ratio_now = ratio_next
    return transform


def kernel(
    n_tok, n_feat,
    e_ref, l_ref, out_ref,
    eall, part, sib, recv, gall, glow, cbuf, ubuf, tbuf, tfull, stat, zstat, fin, halves, outs,
    load_sem, up_sem, down_sem, ag_sem, sib_ssem, sib_rsem, rs_ssem, rs_rsem,
    g_ssem, g_rsem, gl_ssem, gl_rsem, st_ssem, st_rsem, zs_ssem, zs_rsem,
    tg_ssem, tg_rsem, tf_ssem, tf_rsem, fa_ssem, fa_rsem, fb_ssem, fb_rsem,
):
    f32, bf16 = jnp.float32, jnp.bfloat16
    t = lax.axis_index("tok")
    z = lax.axis_index("feat")
    chips = n_tok // 2
    p, c = t // 2, t % 2
    mate = 2 * p + 1 - c
    sub, tokens = e_ref.shape[1:]
    rows = sub * n_tok
    cut = 16 * ((sub // 16 + 1) // 2)
    pieces = [(0, cut), (cut, sub)]
    group = 2 if chips % 2 == 0 else 1
    token_total = tokens * n_tok
    order_all = rows * n_feat
    width = rows // 2

    load = pltpu.make_async_copy(e_ref, eall.at[z], load_sem)
    load.start()

    barrier = pltpu.get_barrier_semaphore()
    for d in range(1, n_tok):
        pl.semaphore_signal(
            barrier, inc=1, device_id=(lax.rem(t + d, n_tok), z), device_id_type=MESH
        )
    for d in range(1, n_feat):
        pl.semaphore_signal(
            barrier, inc=1, device_id=(t, lax.rem(z + d, n_feat)), device_id_type=MESH
        )
    load.wait()
    pl.semaphore_wait(barrier, n_tok + n_feat - 2)

    def remote(src, dst, ssem, rsem, tok, feat):
        return pltpu.make_async_remote_copy(
            src_ref=src, dst_ref=dst, send_sem=ssem, recv_sem=rsem,
            device_id=(tok, feat), device_id_type=MESH,
        )

    def up_copy(r, h):
        at = eall.at[r, :, slice(*pieces[h])]
        return remote(at, at, up_sem.at[r, h], ag_sem.at[r, h], t, z + 1)

    def down_copy(r, h):
        at = eall.at[r, :, slice(*pieces[h])]
        return remote(at, at, down_sem.at[r, h], ag_sem.at[r, h], t, z - 1)

    def sib_copy(r, h):
        at = slice(*pieces[h])
        return remote(
            part.at[r, 1 - c, :, :, at], sib.at[r, :, :, at], sib_ssem.at[r, h],
            sib_rsem.at[r, h], mate, z,
        )

    def rs_copy(r, h, d):
        dest = lax.rem(p + d, chips)
        at = slice(*pieces[h])
        return remote(
            part.at[r, c, dest, :, at], recv.at[d - 1, r, :, at], rs_ssem.at[r, h, d - 1],
            rs_rsem.at[r, h, d - 1], 2 * dest + c, z,
        )

    def g_copy(r, d):
        return remote(
            gall.at[z, r], gall.at[z, r], g_ssem.at[r, d - 1], g_rsem.at[r, d - 1],
            t, lax.rem(z + d, n_feat),
        )

    def gl_copy(d):
        return remote(
            glow.at[z], glow.at[z], gl_ssem.at[d - 1], gl_rsem.at[d - 1],
            t, lax.rem(z + d, n_feat),
        )

    def fetch(r, h, first):
        @pl.when(jnp.logical_not(first))
        def _():
            down_copy(r, h).wait_recv()

        @pl.when(jnp.logical_and(r <= z, z < n_feat - 1))
        def _():
            up_copy(r, h).start()

        @pl.when(jnp.logical_and(r >= z, z > 0))
        def _():
            down_copy(r, h).start()

    def process(r, h):
        lo, hi = pieces[h]
        size = hi - lo
        own_e = e_ref[...].reshape(rows, tokens)

        def chip_rows(k, carry):
            block = eall[r, pl.ds(k * 2 * group, 2 * group), lo:hi, :]
            block = block.reshape(2 * group * size, tokens)
            gram = token_product(block, own_e)
            cross = token_product(block, l_ref[...])
            for g in range(group):
                for core in range(2):
                    at = (2 * g + core) * size
                    part[r, core, k * group + g, 0, lo:hi] = gram[at : at + size]
                    part[r, core, k * group + g, 1, lo:hi] = cross[at : at + size]
            return carry

        lax.fori_loop(0, chips // group, chip_rows, 0)
        sib_copy(r, h).start()

    def finish(r, h):
        lo, hi = pieces[h]
        sib_copy(r, h).wait_recv()

        def add(q, carry):
            part[r, c, q, :, lo:hi] = part[r, c, q, :, lo:hi] + sib[r, q, :, lo:hi]
            return carry

        lax.fori_loop(0, chips, add, 0)
        for d in range(1, chips):
            rs_copy(r, h, d).start()

    def both(s, action):
        @pl.when(z - s >= 0)
        def _():
            action(z - s)

        @pl.when(jnp.logical_and(s > 0, z + s < n_feat))
        def _():
            action(z + s)

    def level(s, carry):
        both(s, lambda r: fetch(r, 0, s == 0))
        both(s, lambda r: process(r, 0))

        @pl.when(s > 0)
        def _():
            both(s - 1, lambda r: finish(r, 1))

        both(s, lambda r: fetch(r, 1, s == 0))
        both(s, lambda r: process(r, 1))
        both(s, lambda r: finish(r, 0))
        return carry

    lax.fori_loop(0, n_feat, level, 0)

    stat[t] = jnp.zeros((8, rows), f32)

    row_id = lax.broadcasted_iota(jnp.int32, (sub, rows), 0)
    col_id = lax.broadcasted_iota(jnp.int32, (sub, rows), 1)
    on_diag = col_id == row_id + t * sub

    def send_gram(r):
        for d in range(1, n_feat):
            g_copy(r, d).start()

    def total(r):
        for h in range(len(pieces)):
            for d in range(1, chips):
                rs_copy(r, h, d).wait_recv()
        both_sum = part[r, c, p]
        for d in range(1, chips):
            both_sum = both_sum + recv[d - 1, r]
        gram = both_sum[0]
        cbuf[r] = both_sum[1] / token_total
        high = gram.astype(bf16)
        gall[z, r] = high

        @pl.when(r == z)
        def _():
            glow[z] = (gram - high.astype(f32)).astype(bf16)


        stat[t, 0:1] += jnp.sum(jnp.abs(gram), axis=0, keepdims=True)
        kept = jnp.where(on_diag, gram, 0.0) * jnp.where(r == z, 1.0, 0.0)
        stat[t, 1:2] += jnp.sum(kept, axis=0, keepdims=True)

    def total_send(r):
        total(r)

    def early(s, carry):
        both(s, total_send)
        return carry

    lax.fori_loop(0, n_feat - 1, early, 0)
    both(n_feat - 1, lambda r: finish(r, 1))
    both(n_feat - 1, total)

    def st_copy(d):
        return remote(
            stat.at[t], stat.at[t], st_ssem.at[d - 1], st_rsem.at[d - 1],
            lax.rem(t + d, n_tok), z,
        )

    def zs_copy(d):
        return remote(
            zstat.at[z], zstat.at[z], zs_ssem.at[d - 1], zs_rsem.at[d - 1],
            t, lax.rem(z + d, n_feat),
        )

    for d in range(1, n_tok):
        st_copy(d).start()
    for d in range(1, n_tok):
        st_copy(d).wait_recv()
    tok_sum = jnp.sum(stat[...], axis=0)
    peak = jnp.max(tok_sum[0:1], axis=1, keepdims=True)
    trace = jnp.sum(tok_sum[1:2], axis=1, keepdims=True)
    zstat[z, 0] = jnp.broadcast_to(peak, (8, 128))
    zstat[z, 1] = jnp.broadcast_to(trace, (8, 128))
    for d in range(1, n_feat):
        zs_copy(d).start()
    for r in range(n_feat):
        send_gram(r)
    for d in range(1, n_feat):
        gl_copy(d).start()
    for d in range(1, n_feat):
        zs_copy(d).wait_recv()
    seen = zstat[...]
    peak_all = jnp.max(seen[:, 0], axis=0)[:1, :1]
    energy = jnp.sum(seen[:, 1], axis=0)[:1, :1]
    ridge_term = ridge_share * energy / (token_total * order_all)
    upper_bound = peak_all / token_total + ridge_term
    center = (upper_bound + ridge_term) / 2.0
    half_span = (upper_bound - ridge_term) / 2.0
    ratio_now = half_span / center

    def start_iterate(r, carry):
        first = cbuf[r] / center
        tbuf[r] = first
        ubuf[r] = first
        tfull[0, r, t] = first.astype(bf16)
        return carry

    lax.fori_loop(0, n_feat, start_iterate, 0)

    beside = p + 1 - 2 * (p % 2)
    across = p + 2 - 4 * (p // 2)
    far = beside + 2 - 4 * (p // 2)
    whole, low_half, high_half = slice(None), slice(0, n_feat // 2), slice(n_feat // 2, n_feat)
    hops = (
        (whole, t, beside), (whole, t, across),
        (low_half, 2 * across + c, beside), (high_half, 2 * beside + c, across),
    )
    shares = (
        (whole, t), (whole, 2 * beside + c), (whole, 2 * across + c),
        (low_half, 2 * far + c), (high_half, 2 * far + c),
    )

    def tg_copy(it, k):
        part_of, tile, dest = hops[k]
        at = tfull.at[it, part_of, tile]
        return remote(at, at, tg_ssem.at[it, k], tg_rsem.at[it, k], 2 * dest + c, z)

    def tf_copy(it, k):
        part_of, tile = shares[k]
        at = tfull.at[it, part_of, tile]
        return remote(at, at, tf_ssem.at[it, k], tf_rsem.at[it, k], mate, z)

    for it in range(ITERS):
        tg_copy(it, 0).start()
        tg_copy(it, 1).start()
        tf_copy(it, 0).start()
        tg_copy(it, 0).wait_recv()
        tg_copy(it, 3).start()
        tf_copy(it, 1).start()
        tg_copy(it, 1).wait_recv()
        tg_copy(it, 2).start()
        tf_copy(it, 2).start()
        tg_copy(it, 2).wait_recv()
        tf_copy(it, 3).start()
        tg_copy(it, 3).wait_recv()
        tf_copy(it, 4).start()
        if it == 0:
            for d in range(1, n_feat):
                for r in range(n_feat):
                    g_copy(r, d).wait_recv()
                gl_copy(d).wait_recv()
        for k in range(len(shares)):
            tf_copy(it, k).wait_recv()
        ratio_next = 1.0 / (2.0 * center / half_span - ratio_now)
        keep = ratio_next * ratio_now
        gain = 2.0 * ratio_next / half_span

        def multiply(k, carry):
            weights = tfull[it, k].reshape(rows, rows)
            left = gall[k].reshape(n_feat * sub, rows)
            product = jnp.dot(left, weights, preferred_element_type=f32)
            low = jnp.dot(glow[k], weights, preferred_element_type=f32)
            product = product.reshape(n_feat, sub, rows)

            @pl.when(k == 0)
            def _():
                fin[...] = product

            @pl.when(k > 0)
            def _():
                fin[...] = fin[...] + product

            recv[0, k, 0] = low
            return carry

        lax.fori_loop(0, n_feat, multiply, 0)

        def advance(r, carry):
            applied = fin[r] + recv[0, r, 0]
            half = tfull[it, r, t].astype(f32)
            residual = cbuf[r] - (applied / token_total + ridge_term * half)
            update = keep * ubuf[r] + gain * residual
            after = tbuf[r] + update
            ubuf[r] = update
            tbuf[r] = after
            if it + 1 < ITERS:
                tfull[it + 1, r, t] = after.astype(bf16)
            return carry

        lax.fori_loop(0, n_feat, advance, 0)
        ratio_now = ratio_next

    def fa_copy(d):
        dest = lax.rem(z + d, n_feat)
        return remote(
            tbuf.at[dest], sib.at[0, z, 0], fa_ssem.at[d - 1], fa_rsem.at[d - 1], t, dest
        )

    def fb_copy(d):
        dest = lax.rem(t + d, n_tok)
        return remote(
            halves.at[dest], outs.at[t], fb_ssem.at[d - 1], fb_rsem.at[d - 1], dest, z
        )

    for d in range(1, n_feat):
        fa_copy(d).start()
    sib[0, z, 0] = tbuf[z]
    for d in range(1, n_feat):
        fa_copy(d).wait_recv()
    for k in range(n_feat):
        tile = sib[0, k, 0]
        halves[2 * k] = tile[:, :width]
        halves[2 * k + 1] = tile[:, width:]
    for d in range(1, n_tok):
        fb_copy(d).start()
    outs[t] = halves[t]
    for d in range(1, n_tok):
        fb_copy(d).wait_recv()
    out_ref[...] = outs[...]

    def drain(r, carry):
        for h in range(len(pieces)):
            @pl.when(jnp.logical_and(r <= z, z < n_feat - 1))
            def _():
                up_copy(r, h).wait_send()

            @pl.when(jnp.logical_and(r >= z, z > 0))
            def _():
                down_copy(r, h).wait_send()

            sib_copy(r, h).wait_send()
            for d in range(1, chips):
                rs_copy(r, h, d).wait_send()
        for d in range(1, n_feat):
            g_copy(r, d).wait_send()
        return carry

    lax.fori_loop(0, n_feat, drain, 0)
    for d in range(1, n_tok):
        st_copy(d).wait_send()
        fb_copy(d).wait_send()
    for d in range(1, n_feat):
        gl_copy(d).wait_send()
        zs_copy(d).wait_send()
        fa_copy(d).wait_send()
    for it in range(ITERS):
        for k in range(len(hops)):
            tg_copy(it, k).wait_send()
        for k in range(len(shares)):
            tf_copy(it, k).wait_send()


def kernel_body(n_tok, n_feat, entering, leaving):
    rows, tokens = entering.shape
    chips, sub, width = n_tok // 2, rows // n_tok, rows // 2
    f32, bf16 = jnp.float32, jnp.bfloat16
    dma = pltpu.SemaphoreType.DMA
    vmem = pltpu.VMEM
    tile = (n_feat, sub, rows)
    out = pl.pallas_call(
        functools.partial(kernel, n_tok, n_feat),
        out_shape=jax.ShapeDtypeStruct((n_tok, sub, width), f32),
        in_specs=[pl.BlockSpec(memory_space=pltpu.VMEM)] * 2,
        out_specs=pl.BlockSpec(memory_space=pltpu.VMEM),
        scratch_shapes=[
            vmem((n_feat, n_tok, sub, tokens), bf16),
            vmem((n_feat, 2, chips, 2, sub, rows), f32),
            vmem((n_feat, chips, 2, sub, rows), f32),
            vmem((chips - 1, n_feat, 2, sub, rows), f32),
            vmem((n_feat, n_feat, sub, rows), bf16),
            vmem((n_feat, sub, rows), bf16),
            vmem(tile, f32),
            vmem(tile, f32),
            vmem(tile, f32),
            vmem((ITERS, n_feat, n_tok, sub, rows), bf16),
            vmem((n_tok, 8, rows), f32),
            vmem((n_feat, 2, 8, 128), f32),
            vmem(tile, f32),
            vmem((n_tok, sub, width), f32),
            vmem((n_tok, sub, width), f32),
            dma,
            dma((n_feat, 2)), dma((n_feat, 2)), dma((n_feat, 2)),
            dma((n_feat, 2)), dma((n_feat, 2)),
            dma((n_feat, 2, chips - 1)), dma((n_feat, 2, chips - 1)),
            dma((n_feat, n_feat - 1)), dma((n_feat, n_feat - 1)),
            dma((n_feat - 1,)), dma((n_feat - 1,)),
            dma((n_tok - 1,)), dma((n_tok - 1,)),
            dma((n_feat - 1,)), dma((n_feat - 1,)),
            dma((ITERS, 4)), dma((ITERS, 4)),
            dma((ITERS, 5)), dma((ITERS, 5)),
            dma((n_feat - 1,)), dma((n_feat - 1,)),
            dma((n_tok - 1,)), dma((n_tok - 1,)),
        ],
        compiler_params=pltpu.CompilerParams(
            collective_id=0, has_side_effects=True, vmem_limit_bytes=VMEM_BYTES
        ),
    )(entering.reshape(n_tok, sub, tokens), leaving)
    return out.reshape(rows, width)


def solution(mesh):
    n_tok, n_feat = mesh.shape["tok"], mesh.shape["feat"]

    def body(entering, leaving):
        rows, tokens = entering.shape
        fits = (
            n_tok == 8
            and n_feat == 4
            and rows % (32 * n_tok) in (0, 16 * n_tok)
            and rows // n_tok > 16
            and rows % 128 == 0
            and tokens % 128 == 0
        )
        if fits:
            return kernel_body(n_tok, n_feat, entering, leaving)
        return plain_body(entering, leaving)

    in_specs = (P("feat", "tok"), P("feat", "tok"))
    out_specs = P("feat", "tok")
    return jax.shard_map(body, mesh=mesh, in_specs=in_specs, out_specs=out_specs, check_vma=False)
```

```python
import functools

import jax
import jax.numpy as jnp
from jax import lax
from jax.experimental import pallas as pl
from jax.experimental.pallas import tpu as pltpu
from jax.sharding import PartitionSpec as P

ITERS = 2

ridge_share = 0.2

MESH = pl.DeviceIdType.MESH
VMEM_BYTES = 64000 * 1024


def token_product(left, right):
    return lax.dot_general(
        left, right, (((1,), (1,)), ((), ())), preferred_element_type=jnp.float32
    )


def plain_body(entering, leaving):
    row_count = entering.shape[0]
    order_all = row_count * lax.axis_size("feat")
    token_total = entering.shape[1] * lax.axis_size("tok")
    gram_piece = token_product(entering, lax.all_gather(entering, "feat", axis=0, tiled=True))
    cross_piece = token_product(entering, lax.all_gather(leaving, "feat", axis=0, tiled=True))
    gram_rows = lax.psum(gram_piece, "tok")
    cross_tile = lax.psum_scatter(cross_piece, "tok", scatter_dimension=1, tiled=True)
    row_peak = jnp.max(jnp.sum(jnp.abs(gram_rows), axis=1))
    own_squares = jnp.sum(jnp.square(entering.astype(jnp.float32)))
    energy = lax.psum(own_squares, ("tok", "feat"))
    peak_all = lax.pmax(row_peak, "feat")
    ridge_term = ridge_share * energy / (token_total * order_all)
    upper_bound = peak_all / token_total + ridge_term
    center = (upper_bound + ridge_term) / 2.0
    half_span = (upper_bound - ridge_term) / 2.0
    target = cross_tile / token_total
    transform = target / center
    update = transform
    ratio_now = half_span / center
    for sweep in range(ITERS):
        iterate_half = transform.astype(jnp.bfloat16)
        applied = jnp.dot(
            gram_rows,
            lax.all_gather(iterate_half, "feat", axis=0, tiled=True).astype(jnp.float32),
            precision=lax.Precision.HIGHEST,
        )
        residual_now = target - (
            applied / token_total + ridge_term * iterate_half.astype(jnp.float32)
        )
        ratio_next = 1.0 / (2.0 * center / half_span - ratio_now)
        update = ratio_next * ratio_now * update + 2.0 * ratio_next / half_span * residual_now
        transform = transform + update
        ratio_now = ratio_next
    return transform


def kernel(
    n_tok, n_feat,
    e_ref, l_ref, out_ref,
    eall, part, sib, recv, gall, glow, cbuf, ubuf, tbuf, tfull, stat, zstat, fin, halves, outs,
    load_sem, up_sem, down_sem, ag_sem, sib_ssem, sib_rsem, rs_ssem, rs_rsem,
    g_ssem, g_rsem, gl_ssem, gl_rsem, st_ssem, st_rsem, zs_ssem, zs_rsem,
    tg_ssem, tg_rsem, tf_ssem, tf_rsem, fa_ssem, fa_rsem, fb_ssem, fb_rsem,
):
    f32, bf16 = jnp.float32, jnp.bfloat16
    t = lax.axis_index("tok")
    z = lax.axis_index("feat")
    chips = n_tok // 2
    p, c = t // 2, t % 2
    mate = 2 * p + 1 - c
    sub, tokens = e_ref.shape[1:]
    rows = sub * n_tok
    cut = 16 * ((sub // 16 + 1) // 2)
    pieces = [(0, cut), (cut, sub)]
    group = 2 if chips % 2 == 0 else 1
    token_total = tokens * n_tok
    order_all = rows * n_feat
    width = rows // 2

    load = pltpu.make_async_copy(e_ref, eall.at[z], load_sem)
    load.start()

    barrier = pltpu.get_barrier_semaphore()
    for d in range(1, n_tok):
        pl.semaphore_signal(
            barrier, inc=1, device_id=(lax.rem(t + d, n_tok), z), device_id_type=MESH
        )
    for d in range(1, n_feat):
        pl.semaphore_signal(
            barrier, inc=1, device_id=(t, lax.rem(z + d, n_feat)), device_id_type=MESH
        )
    load.wait()
    pl.semaphore_wait(barrier, n_tok + n_feat - 2)

    def remote(src, dst, ssem, rsem, tok, feat):
        return pltpu.make_async_remote_copy(
            src_ref=src, dst_ref=dst, send_sem=ssem, recv_sem=rsem,
            device_id=(tok, feat), device_id_type=MESH,
        )

    def up_copy(r, h):
        at = eall.at[r, :, slice(*pieces[h])]
        return remote(at, at, up_sem.at[r, h], ag_sem.at[r, h], t, z + 1)

    def down_copy(r, h):
        at = eall.at[r, :, slice(*pieces[h])]
        return remote(at, at, down_sem.at[r, h], ag_sem.at[r, h], t, z - 1)

    def sib_copy(r, h):
        at = slice(*pieces[h])
        return remote(
            part.at[r, 1 - c, :, :, at], sib.at[r, :, :, at], sib_ssem.at[r, h],
            sib_rsem.at[r, h], mate, z,
        )

    def rs_copy(r, h, d):
        dest = lax.rem(p + d, chips)
        at = slice(*pieces[h])
        return remote(
            part.at[r, c, dest, :, at], recv.at[d - 1, r, :, at], rs_ssem.at[r, h, d - 1],
            rs_rsem.at[r, h, d - 1], 2 * dest + c, z,
        )

    def g_copy(r, d):
        return remote(
            gall.at[z, r], gall.at[z, r], g_ssem.at[r, d - 1], g_rsem.at[r, d - 1],
            t, lax.rem(z + d, n_feat),
        )

    def gl_copy(d):
        return remote(
            glow.at[z], glow.at[z], gl_ssem.at[d - 1], gl_rsem.at[d - 1],
            t, lax.rem(z + d, n_feat),
        )

    def fetch(r, h, first):
        @pl.when(jnp.logical_not(first))
        def _():
            down_copy(r, h).wait_recv()

        @pl.when(jnp.logical_and(r <= z, z < n_feat - 1))
        def _():
            up_copy(r, h).start()

        @pl.when(jnp.logical_and(r >= z, z > 0))
        def _():
            down_copy(r, h).start()

    def process(r, h):
        lo, hi = pieces[h]
        size = hi - lo
        own_e = e_ref[...].reshape(rows, tokens)

        def chip_rows(k, carry):
            block = eall[r, pl.ds(k * 2 * group, 2 * group), lo:hi, :]
            block = block.reshape(2 * group * size, tokens)
            gram = token_product(block, own_e)
            cross = token_product(block, l_ref[...])
            for g in range(group):
                for core in range(2):
                    at = (2 * g + core) * size
                    part[r, core, k * group + g, 0, lo:hi] = gram[at : at + size]
                    part[r, core, k * group + g, 1, lo:hi] = cross[at : at + size]
            return carry

        lax.fori_loop(0, chips // group, chip_rows, 0)
        sib_copy(r, h).start()

    def finish(r, h):
        lo, hi = pieces[h]
        sib_copy(r, h).wait_recv()

        def add(q, carry):
            part[r, c, q, :, lo:hi] = part[r, c, q, :, lo:hi] + sib[r, q, :, lo:hi]
            return carry

        lax.fori_loop(0, chips, add, 0)
        for d in range(1, chips):
            rs_copy(r, h, d).start()

    def both(s, action):
        @pl.when(z - s >= 0)
        def _():
            action(z - s)

        @pl.when(jnp.logical_and(s > 0, z + s < n_feat))
        def _():
            action(z + s)

    def level(s, carry):
        both(s, lambda r: fetch(r, 0, s == 0))
        both(s, lambda r: process(r, 0))

        @pl.when(s > 0)
        def _():
            both(s - 1, lambda r: finish(r, 1))

        both(s, lambda r: fetch(r, 1, s == 0))
        both(s, lambda r: process(r, 1))
        both(s, lambda r: finish(r, 0))
        return carry

    lax.fori_loop(0, n_feat, level, 0)

    stat[t] = jnp.zeros((8, rows), f32)

    row_id = lax.broadcasted_iota(jnp.int32, (sub, rows), 0)
    col_id = lax.broadcasted_iota(jnp.int32, (sub, rows), 1)
    on_diag = col_id == row_id + t * sub

    def send_gram(r):
        for d in range(1, n_feat):
            g_copy(r, d).start()

    def total(r):
        for h in range(len(pieces)):
            for d in range(1, chips):
                rs_copy(r, h, d).wait_recv()
        both_sum = part[r, c, p]
        for d in range(1, chips):
            both_sum = both_sum + recv[d - 1, r]
        gram = both_sum[0]
        cbuf[r] = both_sum[1] / token_total
        high = gram.astype(bf16)
        gall[z, r] = high

        @pl.when(r == z)
        def _():
            glow[z] = (gram - high.astype(f32)).astype(bf16)


        stat[t, 0:1] += jnp.sum(jnp.abs(gram), axis=0, keepdims=True)
        kept = jnp.where(on_diag, gram, 0.0) * jnp.where(r == z, 1.0, 0.0)
        stat[t, 1:2] += jnp.sum(kept, axis=0, keepdims=True)

    def total_send(r):
        total(r)
        send_gram(r)

    def early(s, carry):
        both(s, total_send)
        return carry

    def later(s, carry):
        both(s, total)
        return carry

    lax.fori_loop(0, 2, early, 0)
    lax.fori_loop(2, n_feat - 1, later, 0)
    both(n_feat - 1, lambda r: finish(r, 1))
    both(n_feat - 1, total)

    def st_copy(d):
        return remote(
            stat.at[t], stat.at[t], st_ssem.at[d - 1], st_rsem.at[d - 1],
            lax.rem(t + d, n_tok), z,
        )

    def zs_copy(d):
        return remote(
            zstat.at[z], zstat.at[z], zs_ssem.at[d - 1], zs_rsem.at[d - 1],
            t, lax.rem(z + d, n_feat),
        )

    for d in range(1, n_tok):
        st_copy(d).start()
    for d in range(1, n_tok):
        st_copy(d).wait_recv()
    tok_sum = jnp.sum(stat[...], axis=0)
    peak = jnp.max(tok_sum[0:1], axis=1, keepdims=True)
    trace = jnp.sum(tok_sum[1:2], axis=1, keepdims=True)
    zstat[z, 0] = jnp.broadcast_to(peak, (8, 128))
    zstat[z, 1] = jnp.broadcast_to(trace, (8, 128))
    for d in range(1, n_feat):
        zs_copy(d).start()

    def send_rest(s, carry):
        both(s, send_gram)
        return carry

    lax.fori_loop(2, n_feat, send_rest, 0)
    for d in range(1, n_feat):
        gl_copy(d).start()
    for d in range(1, n_feat):
        zs_copy(d).wait_recv()
    seen = zstat[...]
    peak_all = jnp.max(seen[:, 0], axis=0)[:1, :1]
    energy = jnp.sum(seen[:, 1], axis=0)[:1, :1]
    ridge_term = ridge_share * energy / (token_total * order_all)
    upper_bound = peak_all / token_total + ridge_term
    center = (upper_bound + ridge_term) / 2.0
    half_span = (upper_bound - ridge_term) / 2.0
    ratio_now = half_span / center

    def start_iterate(r, carry):
        first = cbuf[r] / center
        tbuf[r] = first
        ubuf[r] = first
        tfull[0, r, t] = first.astype(bf16)
        return carry

    lax.fori_loop(0, n_feat, start_iterate, 0)

    beside = p + 1 - 2 * (p % 2)
    across = p + 2 - 4 * (p // 2)
    far = beside + 2 - 4 * (p // 2)
    whole, low_half, high_half = slice(None), slice(0, n_feat // 2), slice(n_feat // 2, n_feat)
    hops = (
        (whole, t, beside), (whole, t, across),
        (low_half, 2 * across + c, beside), (high_half, 2 * beside + c, across),
    )
    shares = (
        (whole, t), (whole, 2 * beside + c), (whole, 2 * across + c),
        (low_half, 2 * far + c), (high_half, 2 * far + c),
    )

    def tg_copy(it, k):
        part_of, tile, dest = hops[k]
        at = tfull.at[it, part_of, tile]
        return remote(at, at, tg_ssem.at[it, k], tg_rsem.at[it, k], 2 * dest + c, z)

    def tf_copy(it, k):
        part_of, tile = shares[k]
        at = tfull.at[it, part_of, tile]
        return remote(at, at, tf_ssem.at[it, k], tf_rsem.at[it, k], mate, z)

    for it in range(ITERS):
        tg_copy(it, 0).start()
        tg_copy(it, 1).start()
        tf_copy(it, 0).start()
        tg_copy(it, 0).wait_recv()
        tg_copy(it, 3).start()
        tf_copy(it, 1).start()
        tg_copy(it, 1).wait_recv()
        tg_copy(it, 2).start()
        tf_copy(it, 2).start()
        tg_copy(it, 2).wait_recv()
        tf_copy(it, 3).start()
        tg_copy(it, 3).wait_recv()
        tf_copy(it, 4).start()
        for k in range(len(shares)):
            tf_copy(it, k).wait_recv()
        ratio_next = 1.0 / (2.0 * center / half_span - ratio_now)
        keep = ratio_next * ratio_now
        gain = 2.0 * ratio_next / half_span

        def multiply(d, k):
            weights = tfull[it, k].reshape(rows, rows)
            left = gall[k].reshape(n_feat * sub, rows)
            product = jnp.dot(left, weights, preferred_element_type=f32)
            low = jnp.dot(glow[k], weights, preferred_element_type=f32)
            product = product.reshape(n_feat, sub, rows)

            fin[...] = product if d == 0 else fin[...] + product
            recv[0, k, 0] = low

        for d in range(n_feat):
            if it == 0 and d > 0:
                for r in range(n_feat):
                    g_copy(r, d).wait_recv()
                gl_copy(d).wait_recv()
            multiply(d, lax.rem(z + n_feat - d, n_feat))

        def advance(r, carry):
            applied = fin[r] + recv[0, r, 0]
            half = tfull[it, r, t].astype(f32)
            residual = cbuf[r] - (applied / token_total + ridge_term * half)
            update = keep * ubuf[r] + gain * residual
            after = tbuf[r] + update
            ubuf[r] = update
            tbuf[r] = after
            if it + 1 < ITERS:
                tfull[it + 1, r, t] = after.astype(bf16)
            return carry

        lax.fori_loop(0, n_feat, advance, 0)
        ratio_now = ratio_next

    def fa_copy(d):
        dest = lax.rem(z + d, n_feat)
        return remote(
            tbuf.at[dest], sib.at[0, z, 0], fa_ssem.at[d - 1], fa_rsem.at[d - 1], t, dest
        )

    def fb_to(dest):
        d = lax.rem(dest - t + n_tok, n_tok)
        return remote(
            halves.at[dest], outs.at[t], fb_ssem.at[d - 1], fb_rsem.at[d - 1], dest, z
        )

    def fb_copy(d):
        return fb_to(lax.rem(t + d, n_tok))

    for d in range(1, n_feat):
        fa_copy(d).start()
    sib[0, z, 0] = tbuf[z]
    def split(k):
        tile = sib[0, k, 0]
        halves[2 * k] = tile[:, :width]
        halves[2 * k + 1] = tile[:, width:]
        for core in range(2):
            dest = 2 * k + core

            @pl.when(dest != t)
            def _():
                fb_to(dest).start()

            @pl.when(dest == t)
            def _():
                outs[t] = halves[t]

    split(z)
    for d in range(1, n_feat):
        fa_copy(d).wait_recv()
        split(lax.rem(z + n_feat - d, n_feat))
    for d in range(1, n_tok):
        fb_copy(d).wait_recv()
    out_ref[...] = outs[...]

    def drain(r, carry):
        for h in range(len(pieces)):
            @pl.when(jnp.logical_and(r <= z, z < n_feat - 1))
            def _():
                up_copy(r, h).wait_send()

            @pl.when(jnp.logical_and(r >= z, z > 0))
            def _():
                down_copy(r, h).wait_send()

            sib_copy(r, h).wait_send()
            for d in range(1, chips):
                rs_copy(r, h, d).wait_send()
        for d in range(1, n_feat):
            g_copy(r, d).wait_send()
        return carry

    lax.fori_loop(0, n_feat, drain, 0)
    for d in range(1, n_tok):
        st_copy(d).wait_send()
        fb_copy(d).wait_send()
    for d in range(1, n_feat):
        gl_copy(d).wait_send()
        zs_copy(d).wait_send()
        fa_copy(d).wait_send()
    for it in range(ITERS):
        for k in range(len(hops)):
            tg_copy(it, k).wait_send()
        for k in range(len(shares)):
            tf_copy(it, k).wait_send()


def kernel_body(n_tok, n_feat, entering, leaving):
    rows, tokens = entering.shape
    chips, sub, width = n_tok // 2, rows // n_tok, rows // 2
    f32, bf16 = jnp.float32, jnp.bfloat16
    dma = pltpu.SemaphoreType.DMA
    vmem = pltpu.VMEM
    tile = (n_feat, sub, rows)
    out = pl.pallas_call(
        functools.partial(kernel, n_tok, n_feat),
        out_shape=jax.ShapeDtypeStruct((n_tok, sub, width), f32),
        in_specs=[pl.BlockSpec(memory_space=pltpu.VMEM)] * 2,
        out_specs=pl.BlockSpec(memory_space=pltpu.VMEM),
        scratch_shapes=[
            vmem((n_feat, n_tok, sub, tokens), bf16),
            vmem((n_feat, 2, chips, 2, sub, rows), f32),
            vmem((n_feat, chips, 2, sub, rows), f32),
            vmem((chips - 1, n_feat, 2, sub, rows), f32),
            vmem((n_feat, n_feat, sub, rows), bf16),
            vmem((n_feat, sub, rows), bf16),
            vmem(tile, f32),
            vmem(tile, f32),
            vmem(tile, f32),
            vmem((ITERS, n_feat, n_tok, sub, rows), bf16),
            vmem((n_tok, 8, rows), f32),
            vmem((n_feat, 2, 8, 128), f32),
            vmem(tile, f32),
            vmem((n_tok, sub, width), f32),
            vmem((n_tok, sub, width), f32),
            dma,
            dma((n_feat, 2)), dma((n_feat, 2)), dma((n_feat, 2)),
            dma((n_feat, 2)), dma((n_feat, 2)),
            dma((n_feat, 2, chips - 1)), dma((n_feat, 2, chips - 1)),
            dma((n_feat, n_feat - 1)), dma((n_feat, n_feat - 1)),
            dma((n_feat - 1,)), dma((n_feat - 1,)),
            dma((n_tok - 1,)), dma((n_tok - 1,)),
            dma((n_feat - 1,)), dma((n_feat - 1,)),
            dma((ITERS, 4)), dma((ITERS, 4)),
            dma((ITERS, 5)), dma((ITERS, 5)),
            dma((n_feat - 1,)), dma((n_feat - 1,)),
            dma((n_tok - 1,)), dma((n_tok - 1,)),
        ],
        compiler_params=pltpu.CompilerParams(
            collective_id=0, has_side_effects=True, vmem_limit_bytes=VMEM_BYTES
        ),
    )(entering.reshape(n_tok, sub, tokens), leaving)
    return out.reshape(rows, width)


def solution(mesh):
    n_tok, n_feat = mesh.shape["tok"], mesh.shape["feat"]

    def body(entering, leaving):
        rows, tokens = entering.shape
        fits = (
            n_tok == 8
            and n_feat == 4
            and rows % (32 * n_tok) in (0, 16 * n_tok)
            and rows // n_tok > 16
            and rows % 128 == 0
            and tokens % 128 == 0
        )
        if fits:
            return kernel_body(n_tok, n_feat, entering, leaving)
        return plain_body(entering, leaving)

    in_specs = (P("feat", "tok"), P("feat", "tok"))
    out_specs = P("feat", "tok")
    return jax.shard_map(body, mesh=mesh, in_specs=in_specs, out_specs=out_specs, check_vma=False)
```
